32 devices in a mesh: grp: 2 (over core), dom: 8 (over z, x), sub: 2 (over y).
Axes of the slice: x: 2, y: 2, z: 4, core: 2. Of those that a mesh axis runs over, the one named last changes fastest.
Arguments:
- positions: float32 [3, 8192], P(None, ('grp', 'dom', 'sub')), may hold values from 0 to 4
- charges: float32 [8192], P(('grp', 'dom', 'sub')), may hold values from -3 to 3
- polar: float32 [8192], P(('grp', 'dom', 'sub')), may hold values from 0.1 to 0.6
- features: bfloat16 [8192, 256], P(('grp', 'dom', 'sub')), may hold values from -6 to 6
- neighbours: int32 [8192, 32], P(('grp', 'dom', 'sub')), may hold values from 0 to 512, as said below
- send_rows: int32 [2, 4096], P(None, ('grp', 'dom', 'sub')), may hold values from 0 to 255
- blocks: int32 [128], P(('grp', 'dom', 'sub')), may hold values from 0 to 31
- radial_in: bfloat16 [2, 8, 64], replicated, may hold values from -2 to 2
- radial_mid: bfloat16 [2, 2, 64, 64], replicated, may hold values from -0.75 to 0.75
- radial_out: bfloat16 [2, 64, 256], replicated, may hold values from -0.75 to 0.75
- node_in: bfloat16 [2, 256, 256], replicated, may hold values from -0.375 to 0.375
- node_out: bfloat16 [2, 256, 256], replicated, may hold values from -0.375 to 0.375
- field_gain: float32 [256], replicated, may hold values from -3 to 3
- readout: bfloat16 [256, 2], replicated, may hold values from -0.375 to 0.375
Outputs:
- site_result: float32 [3, 8192], P(None, ('grp', 'dom', 'sub'))
- response: float32 [3, 8192], P(None, ('grp', 'dom', 'sub'))
The draws below stay inside these ranges and needn't reach their ends.
Inputs may be any that keep to these rules, and one draw needn't show every extreme that they name: `neighbours`: entries below 256 name the block's own sites, entries from 256 to 511 its lent sites, 512 an empty slot; empty slots follow the used ones. `blocks`: repeats may occur.
All inputs are finite; a program needn't handle non-finite values.
Results may differ from the reference program's by a relative error of at most 0.0022.
The reference program's roundings to bfloat16 on the way count: a program that leaves them out, or rounds other values in their place, can miss the bound.
Values may be sent and summed in bfloat16 or wider, within the bound.
A program may use at most 64 MiB of HBM per device.

```python
import math
import jax
import jax.numpy as jnp
from jax import lax

CHANNELS = 256
RADIAL = 64
BASIS = 8
NEIGHBOURS = 32
LAYERS = 2
SWEEPS = 4
ROWS = 256
HALO = 128
BLOCK = 128
LISTED = 4
SITES = 8192
RIMS = 4096
LISTS = 128
NBLOCKS = 32
N_DOM = 8
N_SUB = 2


def draw_neighbours(key, part):
    pick_key, count_key, rim_key, side_key = jax.random.split(jax.random.fold_in(key, 17), 4)
    own_pick = jax.random.randint(pick_key, (SITES, NEIGHBOURS), 0, ROWS)
    rim_pick = ROWS + jax.random.randint(rim_key, (SITES, NEIGHBOURS), 0, 2 * HALO)
    coin = jax.random.randint(side_key, (SITES, NEIGHBOURS), 0, 4)
    picked = jnp.where(coin < 3, rim_pick, own_pick)
    counts = jax.random.randint(count_key, (SITES, 1), NEIGHBOURS // 2, NEIGHBOURS + 1)
    slot_index = lax.broadcasted_iota(jnp.int32, (SITES, NEIGHBOURS), 1)
    return jnp.where(slot_index < counts, picked, ROWS + 2 * HALO).astype(jnp.int32)


def with_ends(result, stream_key, low, high):
    longest = result.shape.index(max(result.shape))
    spots = []
    for shift in (0, 1):
        where = [jax.random.randint(jax.random.fold_in(stream_key, axis), (), 0, length) for axis, length in enumerate(result.shape)]
        where[longest] = (where[longest] + shift) % result.shape[longest]
        spots.append(tuple(where))
    return result.at[spots[0]].set(low).at[spots[1]].set(high)


def block_scale(own_key, extent, pieces, smallest, top_value):
    level, own = 1.0, jax.random.fold_in(own_key, 6)
    for position, blocks in pieces:
        heights = jnp.exp(jax.random.uniform(jax.random.fold_in(own, position), (blocks,), jnp.float32, smallest / len(pieces), top_value / len(pieces)))
        level = level * jnp.repeat(heights, extent[position] // blocks).reshape([-1 if axis == position else 1 for axis in range(len(extent))])
    return level


def normal_values(own_key, extent, deviation, reach, pieces=(), kind=jnp.bfloat16):
    values = deviation * jax.random.normal(own_key, extent, jnp.float32)
    if pieces:
        values = values * block_scale(own_key, extent, pieces, -0.22, 0.18)
    return jnp.clip(values, -reach, reach).astype(kind)


def setup_inputs(seed: int = 0) -> dict:
    keys = jax.random.split(jax.random.key(seed), 15)
    return {
        "positions": jnp.clip(4.0 * jax.random.uniform(keys[0], (3, SITES), jnp.float32) ** block_scale(keys[0], (3, SITES), ((1, 32),), -0.2, 0.2), 0.0, 4.0),
        "charges": normal_values(keys[1], (SITES,), 0.5, 3.0, ((0, 32),), jnp.float32),
        "polar": jnp.clip(jnp.exp(math.log(0.6) - 1.7917595 * jax.random.uniform(keys[2], (SITES,), jnp.float32) ** block_scale(keys[2], (SITES,), ((0, 32),), -0.2, 0.2)), 0.1, 0.6),
        "features": normal_values(keys[3], (SITES, CHANNELS), 1.0, 6.0, ((0, 32),)),
        "neighbours": draw_neighbours(jax.random.fold_in(keys[14], 71), 0),
        "send_rows": with_ends(jax.random.randint(keys[5], (2, RIMS), 0, ROWS), jax.random.fold_in(keys[5], 1), 0, ROWS - 1).astype(jnp.int32),
        "blocks": with_ends(jax.random.randint(keys[6], (LISTS,), 0, NBLOCKS), jax.random.fold_in(keys[6], 1), 0, NBLOCKS - 1).astype(jnp.int32),
        "radial_in": normal_values(keys[7], (LAYERS, BASIS, RADIAL), BASIS ** -0.5, 2.0),
        "radial_mid": normal_values(keys[8], (LAYERS, 2, RADIAL, RADIAL), RADIAL ** -0.5, 0.75),
        "radial_out": normal_values(keys[9], (LAYERS, RADIAL, CHANNELS), RADIAL ** -0.5, 0.75),
        "node_in": normal_values(keys[10], (LAYERS, CHANNELS, CHANNELS), CHANNELS ** -0.5, 0.375),
        "node_out": normal_values(keys[11], (LAYERS, CHANNELS, CHANNELS), CHANNELS ** -0.5, 0.375),
        "field_gain": normal_values(keys[12], (CHANNELS,), 0.5, 3.0, (), jnp.float32),
        "readout": normal_values(keys[13], (CHANNELS, 2), CHANNELS ** -0.5, 0.375),
    }


SMOOTH = 1.0
GAMMA = 1.0
SPACING = 0.75

def field_at(target, source, charge, dipole):
    tile_count = target.shape[1] // BLOCK
    tiles = target.reshape(3, tile_count, BLOCK).transpose(1, 0, 2)

    def one_tile(target_tile):
        offset = target_tile[:, :, None] - source[:, None, :]
        dist_sq = lax.optimization_barrier(jnp.sum(offset * offset, axis=0)) + SMOOTH
        inverse = lax.rsqrt(dist_sq)
        inverse_cube = inverse * inverse * inverse
        inverse_fifth = inverse_cube * inverse * inverse
        projected = lax.optimization_barrier(jnp.sum(offset * dipole[:, None, :], axis=0))
        source_scale = charge[None, :] * inverse_cube + 3.0 * projected * inverse_fifth
        return lax.optimization_barrier(jnp.sum(offset * source_scale[None] - dipole[:, None, :] * inverse_cube[None], axis=2))
    return lax.map(one_tile, tiles).transpose(1, 0, 2).reshape(3, -1)

def edge_geometry(local_data, site_table, neighbour_list):
    source = site_table[:3][:, neighbour_list]
    offset = local_data[:3][:, :, None] - source
    dist_sq = lax.optimization_barrier(jnp.sum(offset * offset, axis=0)) + SMOOTH
    return (offset, dist_sq)

def pair_field(offset, dist_sq, source_charge, source_dipole):
    inverse = lax.rsqrt(dist_sq)
    inverse_cube = inverse * inverse * inverse
    inverse_fifth = inverse_cube * inverse * inverse
    projected = lax.optimization_barrier(jnp.sum(offset * source_dipole, axis=0))
    source_scale = source_charge * inverse_cube + 3.0 * projected * inverse_fifth
    return lax.optimization_barrier(jnp.sum(offset * source_scale[None] - source_dipole * inverse_cube[None], axis=2))

def message_update(hidden, lifted_table, radial_basis, neighbour_list, w_first, w_middle, w_last, w_node):
    row_count, channel_count = hidden.shape
    slot_count = neighbour_list.shape[1]
    tile_count = row_count // BLOCK
    basis_tiles = radial_basis.reshape(tile_count, BLOCK * slot_count, radial_basis.shape[2])
    index_tiles = neighbour_list.reshape(tile_count, BLOCK * slot_count)

    def one_tile(operands):
        basis_tile, index_tile = operands
        first_hidden = jax.nn.silu(jnp.dot(basis_tile, w_first, preferred_element_type=jnp.float32)).astype(jnp.bfloat16)
        second_hidden = jax.nn.silu(jnp.dot(first_hidden, w_middle[0], preferred_element_type=jnp.float32)).astype(jnp.bfloat16)
        third_hidden = jax.nn.silu(jnp.dot(second_hidden, w_middle[1], preferred_element_type=jnp.float32)).astype(jnp.bfloat16)
        edge_weight = jnp.dot(third_hidden, w_last, preferred_element_type=jnp.float32)
        source = lifted_table[index_tile].astype(jnp.float32)
        summed = lax.optimization_barrier(jnp.sum((edge_weight * source).reshape(BLOCK, slot_count, channel_count), axis=1))
        return summed / slot_count
    message = lax.map(one_tile, (basis_tiles, index_tiles)).reshape(row_count, channel_count).astype(jnp.bfloat16)
    update = jax.nn.silu(jnp.dot(message, w_node, preferred_element_type=jnp.float32))
    return (hidden.astype(jnp.float32) + update).astype(jnp.bfloat16)

def rim_cols(values, rim_lists):
    to_next = jax.vmap(lambda v, s: v[:, s[0]])(values, rim_lists)
    to_prev = jax.vmap(lambda v, s: v[:, s[1]])(values, rim_lists)
    missing = jnp.zeros_like(to_next[:1])
    lower = jnp.concatenate([missing, to_next[:-1]], 0)
    upper = jnp.concatenate([to_prev[1:], missing], 0)
    empty_entry = jnp.zeros(values.shape[:-1] + (1,), values.dtype)
    return jnp.concatenate([values, lower, upper, empty_entry], -1)

def rim_rows(values, rim_lists):
    to_next = jax.vmap(lambda v, s: v[s[0]])(values, rim_lists)
    to_prev = jax.vmap(lambda v, s: v[s[1]])(values, rim_lists)
    missing = jnp.zeros_like(to_next[:1])
    lower = jnp.concatenate([missing, to_next[:-1]], 0)
    upper = jnp.concatenate([to_prev[1:], missing], 0)
    empty_entry = jnp.zeros((values.shape[0], 1) + values.shape[2:], values.dtype)
    return jnp.concatenate([values, lower, upper, empty_entry], 1)

def reference(positions, charges, polar, features, neighbours, send_rows, blocks, radial_in, radial_mid, radial_out, node_in, node_out, field_gain, readout):
    groups = N_DOM * N_SUB
    local_data = jnp.concatenate([positions, charges[None], polar[None]], 0).reshape(5, 2 * groups, ROWS).transpose(1, 0, 2)
    neighbour_lists = neighbours.reshape(2 * groups, ROWS, NEIGHBOURS)
    rim_lists = send_rows.reshape(2, 2 * groups, HALO).transpose(1, 0, 2)
    block_lists = blocks.reshape(2 * groups, LISTED)
    by_group = local_data.reshape(2, groups, 5, ROWS).transpose(0, 2, 1, 3).reshape(2, 5, groups * ROWS)

    def pick(other, listed):
        return jnp.take(other.reshape(5, -1, BLOCK), listed, axis=1).reshape(5, -1)
    near_learned = jax.vmap(lambda l: pick(by_group[1], l))(block_lists[:groups])
    near_solvent = jax.vmap(lambda l: pick(by_group[0], l))(block_lists[groups:])
    near_sites = jnp.concatenate([near_learned, near_solvent], 0)
    outside = lax.map(lambda a: field_at(a[0][:3], a[1][:3], a[1][3], jnp.zeros_like(a[1][:3])), (local_data, near_sites))
    site_tables = jnp.concatenate([rim_cols(local_data[:groups], rim_lists[:groups]), rim_cols(local_data[groups:], rim_lists[groups:])], 0)
    strength = jnp.sqrt(1.0 + lax.optimization_barrier(jnp.sum(outside * outside, axis=1)))
    learned_offset, learned_dist = jax.vmap(edge_geometry)(local_data[:groups], site_tables[:groups], neighbour_lists[:groups])
    centres = jnp.arange(BASIS, dtype=jnp.float32) * SPACING
    radial_basis = jnp.exp(-GAMMA * (jnp.sqrt(learned_dist)[..., None] - centres) ** 2).astype(jnp.bfloat16)
    initial = features.reshape(2 * groups, ROWS, CHANNELS)[:groups].astype(jnp.float32)
    hidden = (initial + strength[:groups, :, None] * field_gain[None, None, :]).astype(jnp.bfloat16)
    for layer_index in range(LAYERS):
        lifted = lax.map(lambda h: jnp.dot(h, node_in[layer_index], preferred_element_type=jnp.float32).astype(jnp.bfloat16), hidden)
        lifted_tables = rim_rows(lifted, rim_lists[:groups])
        hidden = lax.map(lambda a: message_update(a[0], a[1], a[2], a[3], radial_in[layer_index], radial_mid[layer_index], radial_out[layer_index], node_out[layer_index]), (hidden, lifted_tables, radial_basis, neighbour_lists[:groups]))
    readouts = lax.map(lambda h: jnp.dot(h, readout, preferred_element_type=jnp.float32), hidden)
    solvent_offset, solvent_dist = jax.vmap(edge_geometry)(local_data[groups:], site_tables[groups:], neighbour_lists[groups:])
    source_charge = jax.vmap(lambda t, n: t[3][n])(site_tables[groups:], neighbour_lists[groups:])
    fixed_field = outside[groups:] + jax.vmap(pair_field)(solvent_offset, solvent_dist, source_charge, jnp.zeros_like(solvent_offset))
    polar_rows = local_data[groups:, 4]
    dipole = polar_rows[:, None, :] * fixed_field
    for sweep_index in range(SWEEPS):
        dipole_tables = rim_cols(dipole, rim_lists[groups:])
        gathered = jax.vmap(lambda t, n: t[:, n])(dipole_tables, neighbour_lists[groups:])
        induced = jax.vmap(pair_field)(solvent_offset, solvent_dist, jnp.zeros_like(solvent_dist), gathered)
        dipole = polar_rows[:, None, :] * (fixed_field + induced)
    learned_charge = readouts[:, :, 0]
    source_q = jnp.concatenate([learned_charge, jnp.zeros_like(learned_charge)], 0)
    source_d = jnp.concatenate([jnp.zeros_like(dipole), dipole], 0)
    terms = lax.map(lambda a: field_at(a[0][:3], a[1][:3], a[2], a[3]), (near_sites, local_data, source_q, source_d))

    def collect(part_terms, part_lists):
        flat_terms = part_terms.reshape(groups, 3, LISTED, BLOCK).transpose(1, 0, 2, 3).reshape(3, groups * LISTED, BLOCK)
        summed = jnp.zeros((3, NBLOCKS, BLOCK), jnp.float32).at[:, part_lists.reshape(-1)].add(flat_terms)
        return summed.reshape(3, -1)
    from_learned = collect(terms[:groups], block_lists[:groups])
    from_solvent = collect(terms[groups:], block_lists[groups:])
    response = jnp.concatenate([from_solvent, from_learned], 1)
    learned_rows = jnp.stack([readouts[:, :, 0], readouts[:, :, 1], strength[:groups]], 1)
    site_result = jnp.concatenate([learned_rows, dipole], 0).transpose(1, 0, 2).reshape(3, -1)
    return (site_result, response)
```

```python
import functools

import jax
import jax.numpy as jnp
from jax import lax
from jax.experimental import pallas as pl
from jax.experimental.pallas import tpu as pltpu
from jax.sharding import PartitionSpec as P

SWEEPS = 4
BLOCK = 128
SMOOTH = 1.0
SPACING = 0.75
MESH = pl.DeviceIdType.MESH
F32 = jnp.float32
BF16 = jnp.bfloat16


def silu(x):
    return x * (0.5 + 0.5 * jnp.tanh(0.5 * x))


def lane_pick(rows, index):
    shape = index.shape
    return jnp.take_along_axis(
        jnp.broadcast_to(rows, shape), index, axis=1, mode="promise_in_bounds"
    )


def table_gather(pieces, local, chunk):
    total = jnp.zeros(local.shape, F32)
    for number, rows in pieces:
        total = jnp.where(chunk == number, lane_pick(rows, local), total)
    return total


def kernel(
    n_dom,
    n_sub,
    positions,
    charges,
    polar,
    features,
    neighbours,
    send_rows,
    blocks,
    radial_in,
    radial_mid,
    radial_out,
    node_in,
    node_out,
    field_gain,
    readout,
    site_result,
    response,
    packet,
    everyone,
    near_rows,
    near_cols,
    own_rows,
    own_cols,
    extra_cols,
    rim_out,
    rim_in,
    index_rows,
    geometry,
    hot,
    third,
    wide_in,
    wide_mid,
    wide_out,
    tables,
    lent,
    hidden_ref,
    acc,
    outside,
    term_out,
    term_in,
    all_send,
    all_recv,
    rim_send,
    rim_recv,
    lift_send,
    lift_recv,
    term_send,
    term_recv,
):
    g = lax.axis_index("grp")
    p = lax.axis_index("dom") * n_sub + lax.axis_index("sub")
    n = n_dom * n_sub
    rows = positions.shape[1]
    own_blocks = rows // BLOCK
    slots = neighbours.shape[1]
    listed = blocks.shape[0]
    layers, basis, radial = radial_in.shape
    channels = features.shape[1]
    rim = send_rows.shape[1]
    pack = channels // radial
    groups = slots // pack
    other = 1 - g

    def place(group, q):
        return (group, lax.div(q, n_sub), lax.rem(q, n_sub))

    def peer(i):
        return lax.rem(p + i, n)

    barrier = pltpu.get_barrier_semaphore()

    @pl.loop(0, n)
    def _(i):
        pl.semaphore_signal(barrier, inc=1, device_id=place(other, peer(i)), device_id_type=MESH)

    @pl.when(p > 0)
    def _():
        pl.semaphore_signal(barrier, inc=1, device_id=place(g, p - 1), device_id_type=MESH)

    @pl.when(p < n - 1)
    def _():
        pl.semaphore_signal(barrier, inc=1, device_id=place(g, p + 1), device_id_type=MESH)

    own_rows[...] = jnp.zeros_like(own_rows)
    own_rows[0:3, :] = positions[...]
    own_rows[3:4, :] = charges[...]
    own = own_rows[...]
    for b in range(own_blocks):
        packet[b] = own[:, b * BLOCK : (b + 1) * BLOCK]

    def fill_rims(step, values):
        for side in range(2):
            index = jnp.broadcast_to(send_rows[side : side + 1, :], (8, rim))
            rim_out[step, side] = table_gather(
                [(c, values[:, c * BLOCK : (c + 1) * BLOCK]) for c in range(own_blocks)],
                index & (BLOCK - 1),
                lax.shift_right_logical(index, 7),
            )

    def side_copy(src, dst, send, recv, step, side, q):
        return pltpu.make_async_remote_copy(
            src_ref=src,
            dst_ref=dst,
            send_sem=send.at[step, side],
            recv_sem=recv.at[step, side],
            device_id=place(g, q),
            device_id_type=MESH,
        )

    def rim_copy(step, side, q):
        return side_copy(
            rim_out.at[step, side], rim_in.at[step, side], rim_send, rim_recv, step, side, q
        )

    def lift_copy(layer, side, q):
        return side_copy(
            lent.at[layer, side],
            tables.at[layer, pl.ds(rows + side * rim, rim)],
            lift_send,
            lift_recv,
            layer,
            side,
            q,
        )

    def start(copy, step):
        @pl.when(p < n - 1)
        def _():
            copy(step, 0, p + 1).start()

        @pl.when(p > 0)
        def _():
            copy(step, 1, p - 1).start()

    def arrive(copy, step):
        @pl.when(p > 0)
        def _():
            copy(step, 0, p - 1).wait_recv()

        @pl.when(p < n - 1)
        def _():
            copy(step, 1, p + 1).wait_recv()

    def gone(copy, step):
        @pl.when(p < n - 1)
        def _():
            copy(step, 0, p + 1).wait_send()

        @pl.when(p > 0)
        def _():
            copy(step, 1, p - 1).wait_send()

    fill_rims(0, own)

    @pl.when(p == 0)
    def _():
        for step in range(1 + SWEEPS):
            rim_in[step, 0] = jnp.zeros((8, rim), F32)
        for layer in range(layers):
            tables[layer, rows : rows + rim] = jnp.zeros((rim, channels), BF16)

    @pl.when(p == n - 1)
    def _():
        for step in range(1 + SWEEPS):
            rim_in[step, 1] = jnp.zeros((8, rim), F32)
        for layer in range(layers):
            tables[layer, rows + rim :] = jnp.zeros((rim, channels), BF16)

    pl.semaphore_wait(barrier, n + (p > 0).astype(jnp.int32) + (p < n - 1).astype(jnp.int32))

    def packet_copy(i):
        return pltpu.make_async_remote_copy(
            src_ref=packet,
            dst_ref=everyone.at[pl.ds(p * own_blocks, own_blocks)],
            send_sem=all_send,
            recv_sem=all_recv,
            device_id=place(other, peer(i)),
            device_id_type=MESH,
        )

    start(rim_copy, 0)

    @pl.loop(0, n)
    def _(i):
        packet_copy(i).start()

    wide = jnp.concatenate(
        [neighbours[...].astype(F32), jnp.zeros((rows, BLOCK - slots), F32)], axis=1
    )
    index_rows[...] = wide.T[:slots, :].astype(jnp.int32)
    own_cols[...] = own.T

    @pl.when(g == 0)
    def _():
        lane = lax.broadcasted_iota(jnp.int32, (rows, rows + 2 * rim), 1)
        for k in range(slots):
            hot[k] = jnp.where(neighbours[:, k : k + 1] == lane, 1.0, 0.0).astype(BF16)
        spread_r = (
            lax.broadcasted_iota(jnp.int32, (channels, radial), 0) % radial
            == lax.broadcasted_iota(jnp.int32, (channels, radial), 1)
        ).astype(F32).astype(BF16)
        spread_c = (
            lax.broadcasted_iota(jnp.int32, (radial, channels), 1) % radial
            == lax.broadcasted_iota(jnp.int32, (radial, channels), 0)
        ).astype(F32).astype(BF16)
        same_in = (
            lax.broadcasted_iota(jnp.int32, (pack * basis, channels), 0) // basis
            == lax.broadcasted_iota(jnp.int32, (pack * basis, channels), 1) // radial
        )
        same_mid = (
            lax.broadcasted_iota(jnp.int32, (channels, channels), 0) // radial
            == lax.broadcasted_iota(jnp.int32, (channels, channels), 1) // radial
        )
        for layer in range(layers):
            flat = jnp.dot(radial_in[layer], spread_c, preferred_element_type=F32)
            wide_in[layer] = jnp.where(
                same_in, jnp.concatenate([flat] * pack, axis=0), 0.0
            ).astype(BF16)
            for m in range(2):
                flat = jnp.dot(
                    jnp.dot(spread_r, radial_mid[layer, m], preferred_element_type=F32).astype(
                        BF16
                    ),
                    spread_c,
                    preferred_element_type=F32,
                )
                wide_mid[layer, m] = jnp.where(same_mid, flat, 0.0).astype(BF16)
            for j in range(pack):
                wide_out[layer, j] = jnp.zeros((channels, channels), BF16)
                wide_out[layer, j, j * radial : (j + 1) * radial, :] = radial_out[layer]

    pltpu.make_async_copy(everyone, everyone, all_recv).wait()
    for l in range(listed):
        tile = everyone[blocks[l]]
        near_rows[:, l * BLOCK : (l + 1) * BLOCK] = tile
        near_cols[l * BLOCK : (l + 1) * BLOCK, :] = tile.T

    def field(targets, source_cols, count, charge, dipole):
        x, y, z = (targets[c : c + 1, :] for c in range(3))
        width = targets.shape[1]

        def step(i, sums):
            at = pl.ds(pl.multiple_of(i * 8, 8), 8)
            source = source_cols[at, :]
            rx = x - source[:, 0:1]
            ry = y - source[:, 1:2]
            rz = z - source[:, 2:3]
            w = lax.rsqrt(rx * rx + ry * ry + rz * rz + SMOOTH)
            w2 = w * w
            w3 = w2 * w
            if not dipole:
                s = charge(at, source) * w3
                return (sums[0] + rx * s, sums[1] + ry * s, sums[2] + rz * s)
            d = extra_cols[at, :]
            dx, dy, dz = d[:, 0:1], d[:, 1:2], d[:, 2:3]
            s = 3.0 * (rx * dx + ry * dy + rz * dz) * (w3 * w2)
            return (
                sums[0] + (rx * s - dx * w3),
                sums[1] + (ry * s - dy * w3),
                sums[2] + (rz * s - dz * w3),
            )

        zero = jnp.zeros((8, width), F32)
        sums = lax.fori_loop(0, count // 8, step, (zero, zero, zero), unroll=4)
        return [jnp.sum(s, axis=0, keepdims=True) for s in sums]

    out = field(own, near_cols, listed * BLOCK, lambda at, source: source[:, 3:4], False)
    for c in range(3):
        outside[c : c + 1, :] = out[c]

    def edges():
        arrive(rim_copy, 0)
        for tile in range(own_blocks):
            at = slice(tile * BLOCK, (tile + 1) * BLOCK)
            index = index_rows[:, at]
            local = index & (BLOCK - 1)
            chunk = lax.shift_right_logical(index, 7)
            picked = []
            for c in range(4):
                pieces = [
                    (b, own_rows[c : c + 1, b * BLOCK : (b + 1) * BLOCK])
                    for b in range(own_blocks)
                ] + [(own_blocks + side, rim_in[0, side, c : c + 1, :]) for side in range(2)]
                picked.append(table_gather(pieces, local, chunk))
            ox, oy, oz = (own_rows[c : c + 1, at] - picked[c] for c in range(3))
            dist_sq = ox * ox + oy * oy + oz * oz + SMOOTH
            yield at, (ox, oy, oz), dist_sq, picked[3], local, chunk

    def send_terms(charge, dipole):
        width = listed * BLOCK
        for half in range(0, width, 2 * BLOCK):
            out = field(
                near_rows[:, half : half + 2 * BLOCK], own_cols, rows, charge, dipole
            )
            for c in range(3):
                for l in range(2):
                    term_out[c * listed + half // BLOCK + l] = out[c][
                        0, l * BLOCK : (l + 1) * BLOCK
                    ]

    @pl.when(g == 0)
    def _():
        fx, fy, fz = out
        strength = jnp.sqrt(1.0 + fx * fx + fy * fy + fz * fz)
        site_result[2:3, :] = strength
        strength_col = jnp.broadcast_to(strength, (8, rows)).T[:, 0:1]
        hidden_ref[...] = (features[...].astype(F32) + strength_col * field_gain[...]).astype(BF16)

        def lift(layer):
            lifted = jnp.dot(
                hidden_ref[...], node_in[layer], preferred_element_type=F32
            ).astype(BF16)
            site = lax.broadcasted_iota(jnp.int32, (rows, rim), 0)
            for side in range(2):
                pick = jnp.where(site == send_rows[side : side + 1, :], 1.0, 0.0).astype(BF16)
                lent[layer, side] = lax.dot_general(
                    pick, lifted, (((0,), (0,)), ((), ())), preferred_element_type=F32
                ).astype(BF16)
            start(lift_copy, layer)
            tables[layer, 0:rows] = lifted

        lift(0)
        for at, _, dist_sq, _, _, _ in edges():
            geometry[0, :, at] = jnp.sqrt(dist_sq)

        centre = lax.broadcasted_iota(jnp.int32, (basis, rows), 0).astype(F32) * SPACING

        def radial_step(q, layer):
            parts = []
            for j in range(pack):
                away = jnp.broadcast_to(geometry[0, pl.ds(q * pack + j, 1), :], (basis, rows))
                away = away - centre
                parts.append(jnp.exp(-(away * away)))
            wave = jnp.concatenate(parts, axis=0).astype(BF16)
            h = lax.dot_general(
                wave, wide_in[layer], (((0,), (0,)), ((), ())), preferred_element_type=F32
            )
            h = silu(h).astype(BF16)
            for m in range(2):
                h = silu(jnp.dot(h, wide_mid[layer, m], preferred_element_type=F32)).astype(BF16)
            third[layer, q] = h

        for layer in range(layers):

            @pl.loop(0, groups)
            def _(q):
                radial_step(q, layer)

        for layer in range(layers):
            if layer:
                lift(layer)
            arrive(lift_copy, layer)
            acc[...] = jnp.zeros_like(acc)

            @pl.loop(0, groups)
            def _(q):
                h = third[layer, q]
                table = tables[layer]
                total = None
                for j in range(pack):
                    edge_weight = jnp.dot(h, wide_out[layer, j], preferred_element_type=F32)
                    source = jnp.dot(hot[q * pack + j], table, preferred_element_type=F32)
                    part = edge_weight * source
                    total = part if total is None else total + part
                acc[...] += total

            message = (acc[...] * (1.0 / slots)).astype(BF16)
            update = silu(jnp.dot(message, node_out[layer], preferred_element_type=F32))
            hidden_ref[...] = (hidden_ref[...].astype(F32) + update).astype(BF16)

        readouts = jnp.dot(hidden_ref[...], readout[...], preferred_element_type=F32)
        extra_cols[:, 0:2] = readouts
        padded = jnp.concatenate([readouts, jnp.zeros((rows, BLOCK - 2), F32)], axis=1)
        site_result[0:2, :] = padded.T[0:2, :]
        send_terms(lambda at, source: extra_cols[at, 0:1], False)
        for layer in range(layers):
            gone(lift_copy, layer)

    @pl.when(g == 1)
    def _():
        for at, offset, dist_sq, source_charge, _, _ in edges():
            w = lax.rsqrt(dist_sq)
            w2 = w * w
            w3 = w2 * w
            s = source_charge * w3
            for c in range(3):
                geometry[c, :, at] = offset[c]
                extra = jnp.sum(offset[c] * s, axis=0, keepdims=True)
                outside[c : c + 1, at] = outside[c : c + 1, at] + extra
            geometry[3, :, at] = w3
            geometry[4, :, at] = 3.0 * (w3 * w2)
        gain = polar[...]
        dipole = [gain * outside[c : c + 1, :] for c in range(3)]
        for sweep in range(SWEEPS):
            step = 1 + sweep
            stacked = jnp.concatenate(dipole + [jnp.zeros((5, rows), F32)], axis=0)
            fill_rims(step, stacked)
            start(rim_copy, step)
            arrive(rim_copy, step)
            fresh = [[], [], []]
            for tile in range(own_blocks):
                at = slice(tile * BLOCK, (tile + 1) * BLOCK)
                index = index_rows[:, at]
                local = index & (BLOCK - 1)
                chunk = lax.shift_right_logical(index, 7)
                d = []
                for c in range(3):
                    pieces = [
                        (b, dipole[c][:, b * BLOCK : (b + 1) * BLOCK]) for b in range(own_blocks)
                    ] + [
                        (own_blocks + side, rim_in[step, side, c : c + 1, :]) for side in range(2)
                    ]
                    d.append(table_gather(pieces, local, chunk))
                r = [geometry[c, :, at] for c in range(3)]
                w3 = geometry[3, :, at]
                s = (r[0] * d[0] + r[1] * d[1] + r[2] * d[2]) * geometry[4, :, at]
                for c in range(3):
                    total = jnp.sum(r[c] * s - d[c] * w3, axis=0, keepdims=True)
                    fresh[c].append(gain[:, at] * (outside[c : c + 1, at] + total))
            dipole = [jnp.concatenate(f, axis=1) for f in fresh]
        for c in range(3):
            site_result[c : c + 1, :] = dipole[c]
        stacked = jnp.concatenate(dipole + [jnp.zeros((5, rows), F32)], axis=0)
        extra_cols[...] = stacked.T
        send_terms(None, True)
        for sweep in range(SWEEPS):
            gone(rim_copy, 1 + sweep)

    for l in range(listed):
        term_out[3 * listed + l] = jnp.full((BLOCK,), blocks[l].astype(F32), F32)

    def term_copy(i):
        return pltpu.make_async_remote_copy(
            src_ref=term_out,
            dst_ref=term_in.at[p],
            send_sem=term_send,
            recv_sem=term_recv,
            device_id=place(other, peer(i)),
            device_id_type=MESH,
        )

    @pl.loop(0, n)
    def _(i):
        term_copy(i).start()

    gone(rim_copy, 0)
    pltpu.make_async_copy(everyone, everyone, all_send).wait()
    pltpu.make_async_copy(term_in, term_in, term_recv).wait()

    zero = tuple(jnp.zeros((listed, BLOCK), F32) for _ in range(3 * own_blocks))

    def collect(i, sums):
        terms = term_in[i]
        ids = terms[3 * listed :, :]
        fresh = []
        for b in range(own_blocks):
            mine = (p * own_blocks + b).astype(F32) == ids
            for c in range(3):
                fresh.append(
                    sums[b * 3 + c]
                    + jnp.where(mine, terms[c * listed : (c + 1) * listed, :], 0.0)
                )
        return tuple(fresh)

    sums = lax.fori_loop(0, n, collect, zero)
    for b in range(own_blocks):
        for c in range(3):
            response[c : c + 1, b * BLOCK : (b + 1) * BLOCK] = jnp.sum(
                sums[b * 3 + c], axis=0, keepdims=True
            )
    pltpu.make_async_copy(term_in, term_in, term_send).wait()


def local(n_dom, n_sub, *args):
    (
        positions,
        charges,
        polar,
        features,
        neighbours,
        send_rows,
        blocks,
        radial_in,
        radial_mid,
        radial_out,
        node_in,
        node_out,
        field_gain,
        readout,
    ) = args
    n = n_dom * n_sub
    rows = positions.shape[1]
    own_blocks = rows // BLOCK
    slots = neighbours.shape[1]
    listed = blocks.shape[0]
    layers, basis, radial = radial_in.shape
    channels = features.shape[1]
    rim = send_rows.shape[1]
    pack = channels // radial
    vmem = pl.BlockSpec(memory_space=pltpu.VMEM)
    specs = [vmem] * 14
    specs[6] = pl.BlockSpec(memory_space=pltpu.SMEM)
    dma = pltpu.SemaphoreType.DMA
    return pl.pallas_call(
        functools.partial(kernel, n_dom, n_sub),
        out_shape=(
            jax.ShapeDtypeStruct((3, rows), F32),
            jax.ShapeDtypeStruct((3, rows), F32),
        ),
        in_specs=specs,
        out_specs=(vmem, vmem),
        scratch_shapes=[
            pltpu.VMEM((own_blocks, 8, BLOCK), F32),
            pltpu.VMEM((n * own_blocks, 8, BLOCK), F32),
            pltpu.VMEM((8, listed * BLOCK), F32),
            pltpu.VMEM((listed * BLOCK, 8), F32),
            pltpu.VMEM((8, rows), F32),
            pltpu.VMEM((rows, 8), F32),
            pltpu.VMEM((rows, 8), F32),
            pltpu.VMEM((1 + SWEEPS, 2, 8, rim), F32),
            pltpu.VMEM((1 + SWEEPS, 2, 8, rim), F32),
            pltpu.VMEM((slots, rows), jnp.int32),
            pltpu.VMEM((5, slots, rows), F32),
            pltpu.VMEM((slots, rows, rows + 2 * rim), BF16),
            pltpu.VMEM((layers, slots // pack, rows, channels), BF16),
            pltpu.VMEM((layers, pack * basis, channels), BF16),
            pltpu.VMEM((layers, 2, channels, channels), BF16),
            pltpu.VMEM((layers, pack, channels, channels), BF16),
            pltpu.VMEM((layers, rows + 2 * rim, channels), BF16),
            pltpu.VMEM((layers, 2, rim, channels), BF16),
            pltpu.VMEM((rows, channels), BF16),
            pltpu.VMEM((rows, channels), F32),
            pltpu.VMEM((3, rows), F32),
            pltpu.VMEM((4 * listed, BLOCK), F32),
            pltpu.VMEM((n, 4 * listed, BLOCK), F32),
            dma(()),
            dma(()),
            dma((1 + SWEEPS, 2)),
            dma((1 + SWEEPS, 2)),
            dma((layers, 2)),
            dma((layers, 2)),
            dma(()),
            dma(()),
        ],
        compiler_params=pltpu.CompilerParams(
            collective_id=0, has_side_effects=True, vmem_limit_bytes=56 * 2**20
        ),
    )(
        positions,
        charges.reshape(1, -1),
        polar.reshape(1, -1),
        features,
        neighbours,
        send_rows,
        blocks,
        radial_in,
        radial_mid,
        radial_out,
        node_in,
        node_out,
        field_gain.reshape(1, -1),
        readout,
    )


def solution(mesh):
    sites = ("grp", "dom", "sub")
    in_specs = (
        P(None, sites),
        P(sites),
        P(sites),
        P(sites, None),
        P(sites, None),
        P(None, sites),
        P(sites),
    ) + (P(),) * 7
    out_specs = (P(None, sites), P(None, sites))
    body = functools.partial(local, mesh.shape["dom"], mesh.shape["sub"])
    return jax.shard_map(body, mesh=mesh, in_specs=in_specs, out_specs=out_specs, check_vma=False)
```

```python
import functools

import jax
import jax.numpy as jnp
from jax import lax
from jax.experimental import pallas as pl
from jax.experimental.pallas import tpu as pltpu
from jax.sharding import PartitionSpec as P

SWEEPS = 4
BLOCK = 128
SMOOTH = 1.0
SPACING = 0.75
MESH = pl.DeviceIdType.MESH
F32 = jnp.float32
BF16 = jnp.bfloat16


def silu(x):
    return x * (0.5 + 0.5 * jnp.tanh(0.5 * x))


def lane_pick(rows, index):
    shape = index.shape
    return jnp.take_along_axis(
        jnp.broadcast_to(rows, shape), index, axis=1, mode="promise_in_bounds"
    )


def table_gather(pieces, local, chunk):
    total = jnp.zeros(local.shape, F32)
    for number, rows in pieces:
        total = jnp.where(chunk == number, lane_pick(rows, local), total)
    return total


def kernel(
    n_dom,
    n_sub,
    positions,
    charges,
    polar,
    features,
    neighbours,
    send_rows,
    blocks,
    radial_in,
    radial_mid,
    radial_out,
    node_in,
    node_out,
    field_gain,
    readout,
    both,
    packet,
    everyone,
    near_rows,
    near_cols,
    own_rows,
    own_cols,
    extra_cols,
    rim_out,
    rim_in,
    geometry,
    hot,
    third,
    edge_weight,
    wide_in,
    wide_mid,
    wide_out,
    tables,
    lent,
    hidden_ref,
    acc,
    outside,
    pairs,
    terms,
    term_out,
    term_in,
    all_send,
    all_recv,
    rim_send,
    rim_recv,
    lift_send,
    lift_recv,
    term_send,
    term_recv,
):
    g = lax.axis_index("grp")
    p = lax.axis_index("dom") * n_sub + lax.axis_index("sub")
    site_result, response = both.at[0], both.at[1]
    n = n_dom * n_sub
    rows = positions.shape[1]
    own_blocks = rows // BLOCK
    slots = neighbours.shape[0]
    listed = blocks.shape[0]
    layers, basis, radial = radial_in.shape
    channels = features.shape[1]
    rim = send_rows.shape[1]
    pack = channels // radial
    groups = slots // pack
    other = 1 - g

    def place(group, q):
        return (group, lax.div(q, n_sub), lax.rem(q, n_sub))

    def peer(i):
        return lax.rem(p + i, n)

    barrier = pltpu.get_barrier_semaphore()

    @pl.loop(0, n)
    def _(i):
        pl.semaphore_signal(barrier, inc=1, device_id=place(other, peer(i)), device_id_type=MESH)

    @pl.when(p > 0)
    def _():
        pl.semaphore_signal(barrier, inc=1, device_id=place(g, p - 1), device_id_type=MESH)

    @pl.when(p < n - 1)
    def _():
        pl.semaphore_signal(barrier, inc=1, device_id=place(g, p + 1), device_id_type=MESH)

    own_rows[...] = jnp.zeros_like(own_rows)
    own_rows[0:3, :] = positions[...]
    own_rows[3:4, :] = charges[...]
    own = own_rows[...]
    for b in range(own_blocks):
        packet[b] = own[:, b * BLOCK : (b + 1) * BLOCK]

    def fill_rims(step, values):
        for side in range(2):
            index = jnp.broadcast_to(send_rows[side : side + 1, :], (8, rim))
            rim_out[step, side] = table_gather(
                [(c, values[:, c * BLOCK : (c + 1) * BLOCK]) for c in range(own_blocks)],
                index & (BLOCK - 1),
                lax.shift_right_logical(index, 7),
            )

    def side_copy(src, dst, send, recv, step, side, q):
        return pltpu.make_async_remote_copy(
            src_ref=src,
            dst_ref=dst,
            send_sem=send.at[step, side],
            recv_sem=recv.at[step, side],
            device_id=place(g, q),
            device_id_type=MESH,
        )

    def rim_copy(step, side, q):
        return side_copy(
            rim_out.at[step, side], rim_in.at[step, side], rim_send, rim_recv, step, side, q
        )

    def lift_copy(layer, side, q):
        return side_copy(
            lent.at[layer, side],
            tables.at[layer, pl.ds(rows + side * rim, rim)],
            lift_send,
            lift_recv,
            layer,
            side,
            q,
        )

    def start(copy, step):
        @pl.when(p < n - 1)
        def _():
            copy(step, 0, p + 1).start()

        @pl.when(p > 0)
        def _():
            copy(step, 1, p - 1).start()

    def arrive(copy, step):
        @pl.when(p > 0)
        def _():
            copy(step, 0, p - 1).wait_recv()

        @pl.when(p < n - 1)
        def _():
            copy(step, 1, p + 1).wait_recv()

    def gone(copy, step):
        @pl.when(p < n - 1)
        def _():
            copy(step, 0, p + 1).wait_send()

        @pl.when(p > 0)
        def _():
            copy(step, 1, p - 1).wait_send()

    fill_rims(0, own)

    @pl.when(p == 0)
    def _():
        for step in range(1 + SWEEPS):
            rim_in[step, 0] = jnp.zeros((8, rim), F32)
        for layer in range(layers):
            tables[layer, rows : rows + rim] = jnp.zeros((rim, channels), BF16)

    @pl.when(p == n - 1)
    def _():
        for step in range(1 + SWEEPS):
            rim_in[step, 1] = jnp.zeros((8, rim), F32)
        for layer in range(layers):
            tables[layer, rows + rim :] = jnp.zeros((rim, channels), BF16)

    pl.semaphore_wait(barrier, n + (p > 0).astype(jnp.int32) + (p < n - 1).astype(jnp.int32))

    def packet_copy(i):
        return pltpu.make_async_remote_copy(
            src_ref=packet,
            dst_ref=everyone.at[pl.ds(p * own_blocks, own_blocks)],
            send_sem=all_send,
            recv_sem=all_recv,
            device_id=place(other, peer(i)),
            device_id_type=MESH,
        )

    start(rim_copy, 0)

    @pl.loop(0, n)
    def _(i):
        packet_copy(i).start()

    own_cols[...] = own.T

    def field(targets, source_cols, count, charge, dipole):
        x, y, z = (targets[c : c + 1, :] for c in range(3))
        width = targets.shape[1]

        def step(i, sums):
            at = pl.ds(pl.multiple_of(i * 8, 8), 8)
            source = source_cols[at, :]
            rx = x - source[:, 0:1]
            ry = y - source[:, 1:2]
            rz = z - source[:, 2:3]
            w = lax.rsqrt(rx * rx + ry * ry + rz * rz + SMOOTH)
            w2 = w * w
            w3 = w2 * w
            if not dipole:
                s = charge(at, source) * w3
                return (sums[0] + rx * s, sums[1] + ry * s, sums[2] + rz * s)
            d = extra_cols[at, :]
            dx, dy, dz = d[:, 0:1], d[:, 1:2], d[:, 2:3]
            s = 3.0 * (rx * dx + ry * dy + rz * dz) * (w3 * w2)
            return (
                sums[0] + (rx * s - dx * w3),
                sums[1] + (ry * s - dy * w3),
                sums[2] + (rz * s - dz * w3),
            )

        zero = jnp.zeros((8, width), F32)
        sums = lax.fori_loop(0, count // 8, step, (zero, zero, zero), unroll=16)
        return [jnp.sum(s, axis=0, keepdims=True) for s in sums]

    def edges():
        arrive(rim_copy, 0)
        for tile in range(own_blocks):
            at = slice(tile * BLOCK, (tile + 1) * BLOCK)
            index = neighbours[:, at]
            local = index & (BLOCK - 1)
            chunk = lax.shift_right_logical(index, 7)
            picked = []
            for c in range(4):
                pieces = [
                    (b, own_rows[c : c + 1, b * BLOCK : (b + 1) * BLOCK])
                    for b in range(own_blocks)
                ] + [(own_blocks + side, rim_in[0, side, c : c + 1, :]) for side in range(2)]
                picked.append(table_gather(pieces, local, chunk))
            ox, oy, oz = (own_rows[c : c + 1, at] - picked[c] for c in range(3))
            dist_sq = ox * ox + oy * oy + oz * oz + SMOOTH
            yield at, (ox, oy, oz), dist_sq, picked[3], local, chunk

    def send_terms(charge, dipole):
        width = listed * BLOCK
        for half in range(0, width, 2 * BLOCK):
            out = field(
                near_rows[:, half : half + 2 * BLOCK], own_cols, rows, charge, dipole
            )
            for c in range(3):
                terms[c : c + 1, half : half + 2 * BLOCK] = out[c]

    centre = lax.broadcasted_iota(jnp.int32, (basis, rows), 0).astype(F32) * SPACING

    def radial_step(q, layer):
        parts = []
        for j in range(pack):
            away = jnp.broadcast_to(geometry[0, pl.ds(q * pack + j, 1), :], (basis, rows))
            away = away - centre
            parts.append(jnp.exp(-(away * away)))
        wave = jnp.concatenate(parts, axis=0).astype(BF16)
        h = lax.dot_general(
            wave, wide_in[layer], (((0,), (0,)), ((), ())), preferred_element_type=F32
        )
        h = silu(h).astype(BF16)
        for m in range(2):
            h = silu(jnp.dot(h, wide_mid[layer, m], preferred_element_type=F32)).astype(BF16)
        third[layer, q] = h

    def radial_net(layer):
        @pl.loop(0, groups)
        def _(q):
            radial_step(q, layer)

    def edge_net(layer):
        @pl.loop(0, pack)
        def _(j):
            weight = jnp.dot(
                third[layer].reshape(groups * rows, channels),
                wide_out[layer, j],
                preferred_element_type=F32,
            )
            edge_weight[j] = weight.reshape(groups, rows, channels)

    @pl.when(g == 0)
    def _():
        lane = lax.broadcasted_iota(jnp.int32, (rows, rows + 2 * rim), 1)
        listing = jnp.concatenate(
            [neighbours[...].astype(F32), jnp.zeros((BLOCK - slots, rows), F32)], axis=0
        ).T.astype(jnp.int32)
        for k in range(slots):
            hot[k % pack, k // pack] = jnp.where(listing[:, k : k + 1] == lane, 1.0, 0.0).astype(BF16)
        spread_r = (
            lax.broadcasted_iota(jnp.int32, (channels, radial), 0) % radial
            == lax.broadcasted_iota(jnp.int32, (channels, radial), 1)
        ).astype(F32).astype(BF16)
        spread_c = (
            lax.broadcasted_iota(jnp.int32, (radial, channels), 1) % radial
            == lax.broadcasted_iota(jnp.int32, (radial, channels), 0)
        ).astype(F32).astype(BF16)
        same_in = (
            lax.broadcasted_iota(jnp.int32, (pack * basis, channels), 0) // basis
            == lax.broadcasted_iota(jnp.int32, (pack * basis, channels), 1) // radial
        )
        same_mid = (
            lax.broadcasted_iota(jnp.int32, (channels, channels), 0) // radial
            == lax.broadcasted_iota(jnp.int32, (channels, channels), 1) // radial
        )
        for layer in range(layers):
            flat = jnp.dot(radial_in[layer], spread_c, preferred_element_type=F32)
            wide_in[layer] = jnp.where(
                same_in, jnp.concatenate([flat] * pack, axis=0), 0.0
            ).astype(BF16)
            for m in range(2):
                flat = jnp.dot(
                    jnp.dot(spread_r, radial_mid[layer, m], preferred_element_type=F32).astype(
                        BF16
                    ),
                    spread_c,
                    preferred_element_type=F32,
                )
                wide_mid[layer, m] = jnp.where(same_mid, flat, 0.0).astype(BF16)
            for j in range(pack):
                wide_out[layer, j] = jnp.zeros((channels, channels), BF16)
                wide_out[layer, j, j * radial : (j + 1) * radial, :] = radial_out[layer]
        for at, _, dist_sq, _, _, _ in edges():
            geometry[0, :, at] = jnp.sqrt(dist_sq)
        radial_net(0)

    @pl.when(g == 1)
    def _():
        for at, offset, dist_sq, source_charge, _, _ in edges():
            w = lax.rsqrt(dist_sq)
            w2 = w * w
            w3 = w2 * w
            s = source_charge * w3
            for c in range(3):
                geometry[c, :, at] = offset[c]
                extra = jnp.sum(offset[c] * s, axis=0, keepdims=True)
                pairs[c : c + 1, at] = extra
            geometry[3, :, at] = w3
            geometry[4, :, at] = 3.0 * (w3 * w2)

    pltpu.make_async_copy(everyone, everyone, all_recv).wait()
    for l in range(listed):
        tile = everyone[blocks[l]]
        near_rows[:, l * BLOCK : (l + 1) * BLOCK] = tile
        near_cols[l * BLOCK : (l + 1) * BLOCK, :] = tile.T

    out = field(own, near_cols, listed * BLOCK, lambda at, source: source[:, 3:4], False)
    for c in range(3):
        outside[c : c + 1, :] = out[c]

    @pl.when(g == 0)
    def _():
        fx, fy, fz = out
        strength = jnp.sqrt(1.0 + fx * fx + fy * fy + fz * fz)
        site_result[2:3, :] = strength
        strength_col = jnp.broadcast_to(strength, (8, rows)).T[:, 0:1]
        hidden_ref[...] = (features[...].astype(F32) + strength_col * field_gain[...]).astype(BF16)

        def lift(layer):
            lifted = jnp.dot(
                hidden_ref[...], node_in[layer], preferred_element_type=F32
            ).astype(BF16)
            site = lax.broadcasted_iota(jnp.int32, (rows, rim), 0)
            for side in range(2):
                pick = jnp.where(site == send_rows[side : side + 1, :], 1.0, 0.0).astype(BF16)
                lent[layer, side] = lax.dot_general(
                    pick, lifted, (((0,), (0,)), ((), ())), preferred_element_type=F32
                ).astype(BF16)
            start(lift_copy, layer)
            tables[layer, 0:rows] = lifted

        for layer in range(layers):
            lift(layer)
            edge_net(layer)
            if layer + 1 < layers:
                radial_net(layer + 1)
            arrive(lift_copy, layer)
            acc[...] = jnp.zeros_like(acc)

            @pl.loop(0, pack)
            def _(j):
                source = jnp.dot(
                    hot[j].reshape(groups * rows, rows + 2 * rim),
                    tables[layer],
                    preferred_element_type=F32,
                )
                product = edge_weight[j] * source.reshape(groups, rows, channels)
                acc[...] += jnp.sum(product, axis=0)

            message = (acc[...] * (1.0 / slots)).astype(BF16)
            update = silu(jnp.dot(message, node_out[layer], preferred_element_type=F32))
            hidden_ref[...] = (hidden_ref[...].astype(F32) + update).astype(BF16)

        across = (((1,), (1,)), ((), ()))
        extra_cols[:, 0:2] = lax.dot_general(
            hidden_ref[...], readout[...], across, preferred_element_type=F32
        )
        site_result[0:2, :] = lax.dot_general(
            readout[...], hidden_ref[...], across, preferred_element_type=F32
        )
        send_terms(lambda at, source: extra_cols[at, 0:1], False)
        for layer in range(layers):
            gone(lift_copy, layer)

    @pl.when(g == 1)
    def _():
        gain = polar[...]
        outside[...] = outside[...] + pairs[...]
        dipole = [gain * outside[c : c + 1, :] for c in range(3)]
        for sweep in range(SWEEPS):
            step = 1 + sweep
            stacked = jnp.concatenate(dipole + [jnp.zeros((5, rows), F32)], axis=0)
            fill_rims(step, stacked)
            start(rim_copy, step)
            arrive(rim_copy, step)
            fresh = [[], [], []]
            for tile in range(own_blocks):
                at = slice(tile * BLOCK, (tile + 1) * BLOCK)
                index = neighbours[:, at]
                local = index & (BLOCK - 1)
                chunk = lax.shift_right_logical(index, 7)
                d = []
                for c in range(3):
                    pieces = [
                        (b, dipole[c][:, b * BLOCK : (b + 1) * BLOCK]) for b in range(own_blocks)
                    ] + [
                        (own_blocks + side, rim_in[step, side, c : c + 1, :]) for side in range(2)
                    ]
                    d.append(table_gather(pieces, local, chunk))
                r = [geometry[c, :, at] for c in range(3)]
                w3 = geometry[3, :, at]
                s = (r[0] * d[0] + r[1] * d[1] + r[2] * d[2]) * geometry[4, :, at]
                for c in range(3):
                    total = jnp.sum(r[c] * s - d[c] * w3, axis=0, keepdims=True)
                    fresh[c].append(gain[:, at] * (outside[c : c + 1, at] + total))
            dipole = [jnp.concatenate(f, axis=1) for f in fresh]
        for c in range(3):
            site_result[c : c + 1, :] = dipole[c]
        stacked = jnp.concatenate(dipole + [jnp.zeros((5, rows), F32)], axis=0)
        extra_cols[...] = stacked.T
        send_terms(None, True)
        for sweep in range(SWEEPS):
            gone(rim_copy, 1 + sweep)

    @pl.loop(0, n)
    def _(q):
        for b in range(own_blocks):
            total = jnp.zeros((3, BLOCK), F32)
            for l in range(listed):
                total = total + jnp.where(
                    blocks[l] == q * own_blocks + b, terms[:, l * BLOCK : (l + 1) * BLOCK], 0.0
                )
            term_out[q, b * 3 : (b + 1) * 3, :] = total

    def term_copy(i):
        return pltpu.make_async_remote_copy(
            src_ref=term_out.at[peer(i)],
            dst_ref=term_in.at[p],
            send_sem=term_send,
            recv_sem=term_recv,
            device_id=place(other, peer(i)),
            device_id_type=MESH,
        )

    @pl.loop(0, n)
    def _(i):
        term_copy(i).start()

    gone(rim_copy, 0)
    pltpu.make_async_copy(everyone, everyone, all_send).wait()
    pltpu.make_async_copy(term_in, term_in, term_recv).wait()

    total = jnp.sum(term_in[...], axis=0)
    for b in range(own_blocks):
        response[:, b * BLOCK : (b + 1) * BLOCK] = total[b * 3 : (b + 1) * 3, :]
    pltpu.make_async_copy(term_in, term_in, term_send).wait()


def local(n_dom, n_sub, *args):
    (
        positions,
        charges,
        polar,
        features,
        neighbours,
        send_rows,
        blocks,
        radial_in,
        radial_mid,
        radial_out,
        node_in,
        node_out,
        field_gain,
        readout,
    ) = args
    n = n_dom * n_sub
    rows = positions.shape[1]
    own_blocks = rows // BLOCK
    slots = neighbours.shape[1]
    listed = blocks.shape[0]
    layers, basis, radial = radial_in.shape
    channels = features.shape[1]
    rim = send_rows.shape[1]
    pack = channels // radial
    vmem = pl.BlockSpec(memory_space=pltpu.VMEM)
    specs = [vmem] * 14
    specs[6] = pl.BlockSpec(memory_space=pltpu.SMEM)
    dma = pltpu.SemaphoreType.DMA
    both = pl.pallas_call(
        functools.partial(kernel, n_dom, n_sub),
        out_shape=jax.ShapeDtypeStruct((2, 3, rows), F32),
        in_specs=specs,
        out_specs=vmem,
        scratch_shapes=[
            pltpu.VMEM((own_blocks, 8, BLOCK), F32),
            pltpu.VMEM((n * own_blocks, 8, BLOCK), F32),
            pltpu.VMEM((8, listed * BLOCK), F32),
            pltpu.VMEM((listed * BLOCK, 8), F32),
            pltpu.VMEM((8, rows), F32),
            pltpu.VMEM((rows, 8), F32),
            pltpu.VMEM((rows, 8), F32),
            pltpu.VMEM((1 + SWEEPS, 2, 8, rim), F32),
            pltpu.VMEM((1 + SWEEPS, 2, 8, rim), F32),
            pltpu.VMEM((5, slots, rows), F32),
            pltpu.VMEM((pack, slots // pack, rows, rows + 2 * rim), BF16),
            pltpu.VMEM((layers, slots // pack, rows, channels), BF16),
            pltpu.VMEM((pack, slots // pack, rows, channels), F32),
            pltpu.VMEM((layers, pack * basis, channels), BF16),
            pltpu.VMEM((layers, 2, channels, channels), BF16),
            pltpu.VMEM((layers, pack, channels, channels), BF16),
            pltpu.VMEM((layers, rows + 2 * rim, channels), BF16),
            pltpu.VMEM((layers, 2, rim, channels), BF16),
            pltpu.VMEM((rows, channels), BF16),
            pltpu.VMEM((rows, channels), F32),
            pltpu.VMEM((3, rows), F32),
            pltpu.VMEM((3, rows), F32),
            pltpu.VMEM((3, listed * BLOCK), F32),
            pltpu.VMEM((n, own_blocks * 3, BLOCK), F32),
            pltpu.VMEM((n, own_blocks * 3, BLOCK), F32),
            dma(()),
            dma(()),
            dma((1 + SWEEPS, 2)),
            dma((1 + SWEEPS, 2)),
            dma((layers, 2)),
            dma((layers, 2)),
            dma(()),
            dma(()),
        ],
        compiler_params=pltpu.CompilerParams(
            collective_id=0, has_side_effects=True, vmem_limit_bytes=56 * 2**20
        ),
    )(
        positions,
        charges.reshape(1, -1),
        polar.reshape(1, -1),
        features,
        neighbours.T,
        send_rows,
        blocks,
        radial_in,
        radial_mid,
        radial_out,
        node_in,
        node_out,
        field_gain.reshape(1, -1),
        readout.T,
    )
    return both[0], both[1]


def solution(mesh):
    sites = ("grp", "dom", "sub")
    in_specs = (
        P(None, sites),
        P(sites),
        P(sites),
        P(sites, None),
        P(sites, None),
        P(None, sites),
        P(sites),
    ) + (P(),) * 7
    out_specs = (P(None, sites), P(None, sites))
    body = functools.partial(local, mesh.shape["dom"], mesh.shape["sub"])
    return jax.shard_map(body, mesh=mesh, in_specs=in_specs, out_specs=out_specs, check_vma=False)
```

```python
import functools

import jax
import jax.numpy as jnp
from jax import lax
from jax.experimental import pallas as pl
from jax.experimental.pallas import tpu as pltpu
from jax.sharding import PartitionSpec as P

SWEEPS = 4
BLOCK = 128
SMOOTH = 1.0
SPACING = 0.75
MESH = pl.DeviceIdType.MESH
F32 = jnp.float32
BF16 = jnp.bfloat16


def silu(x):
    return x * (0.5 + 0.5 * jnp.tanh(0.5 * x))


def lane_pick(rows, index):
    shape = index.shape
    return jnp.take_along_axis(
        jnp.broadcast_to(rows, shape), index, axis=1, mode="promise_in_bounds"
    )


def table_gather(pieces, local, chunk):
    total = jnp.zeros(local.shape, F32)
    for number, rows in pieces:
        total = jnp.where(chunk == number, lane_pick(rows, local), total)
    return total


def kernel(
    n_dom,
    n_sub,
    positions,
    charges,
    polar,
    features,
    neighbours,
    send_rows,
    blocks,
    radial_in,
    radial_mid,
    radial_out,
    node_in,
    node_out,
    field_gain,
    readout,
    both,
    packet,
    everyone,
    near_rows,
    near_cols,
    own_rows,
    own_cols,
    extra_cols,
    rim_out,
    rim_in,
    geometry,
    hot,
    third,
    edge_weight,
    wide_in,
    wide_mid,
    wide_out,
    tables,
    lent,
    hidden_ref,
    acc,
    outside,
    pairs,
    terms,
    term_out,
    term_in,
    all_send,
    all_recv,
    rim_send,
    rim_recv,
    lift_send,
    lift_recv,
    term_send,
    term_recv,
):
    g = lax.axis_index("grp")
    p = lax.axis_index("dom") * n_sub + lax.axis_index("sub")
    site_result, response = both.at[0], both.at[1]
    n = n_dom * n_sub
    rows = positions.shape[1]
    own_blocks = rows // BLOCK
    slots = neighbours.shape[0]
    listed = blocks.shape[0]
    layers, basis, radial = radial_in.shape
    channels = features.shape[1]
    rim = send_rows.shape[1]
    pack = channels // radial
    groups = slots // pack
    other = 1 - g

    def place(group, q):
        return (group, lax.div(q, n_sub), lax.rem(q, n_sub))

    def peer(i):
        return lax.rem(p + i, n)

    barrier = pltpu.get_barrier_semaphore()

    @pl.loop(0, n)
    def _(i):
        pl.semaphore_signal(barrier, inc=1, device_id=place(other, peer(i)), device_id_type=MESH)

    @pl.when(p > 0)
    def _():
        pl.semaphore_signal(barrier, inc=1, device_id=place(g, p - 1), device_id_type=MESH)

    @pl.when(p < n - 1)
    def _():
        pl.semaphore_signal(barrier, inc=1, device_id=place(g, p + 1), device_id_type=MESH)

    own_rows[...] = jnp.zeros_like(own_rows)
    own_rows[0:3, :] = positions[...]
    own_rows[3:4, :] = charges[...]
    own = own_rows[...]
    for b in range(own_blocks):
        packet[b] = own[:, b * BLOCK : (b + 1) * BLOCK]

    def fill_rims(step, values):
        for side in range(2):
            index = jnp.broadcast_to(send_rows[side : side + 1, :], (8, rim))
            rim_out[step, side] = table_gather(
                [(c, values[:, c * BLOCK : (c + 1) * BLOCK]) for c in range(own_blocks)],
                index & (BLOCK - 1),
                lax.shift_right_logical(index, 7),
            )

    def side_copy(src, dst, send, recv, step, side, q):
        return pltpu.make_async_remote_copy(
            src_ref=src,
            dst_ref=dst,
            send_sem=send.at[step, side],
            recv_sem=recv.at[step, side],
            device_id=place(g, q),
            device_id_type=MESH,
        )

    def rim_copy(step, side, q):
        return side_copy(
            rim_out.at[step, side], rim_in.at[step, side], rim_send, rim_recv, step, side, q
        )

    def lift_copy(layer, side, q):
        return side_copy(
            lent.at[layer, side],
            tables.at[layer, pl.ds(rows + side * rim, rim)],
            lift_send,
            lift_recv,
            layer,
            side,
            q,
        )

    def start(copy, step):
        @pl.when(p < n - 1)
        def _():
            copy(step, 0, p + 1).start()

        @pl.when(p > 0)
        def _():
            copy(step, 1, p - 1).start()

    def arrive(copy, step):
        @pl.when(p > 0)
        def _():
            copy(step, 0, p - 1).wait_recv()

        @pl.when(p < n - 1)
        def _():
            copy(step, 1, p + 1).wait_recv()

    def gone(copy, step):
        @pl.when(p < n - 1)
        def _():
            copy(step, 0, p + 1).wait_send()

        @pl.when(p > 0)
        def _():
            copy(step, 1, p - 1).wait_send()

    fill_rims(0, own)

    @pl.when(p == 0)
    def _():
        for step in range(1 + SWEEPS):
            rim_in[step, 0] = jnp.zeros((8, rim), F32)
        for layer in range(layers):
            tables[layer, rows : rows + rim] = jnp.zeros((rim, channels), BF16)

    @pl.when(p == n - 1)
    def _():
        for step in range(1 + SWEEPS):
            rim_in[step, 1] = jnp.zeros((8, rim), F32)
        for layer in range(layers):
            tables[layer, rows + rim :] = jnp.zeros((rim, channels), BF16)

    pl.semaphore_wait(barrier, n + (p > 0).astype(jnp.int32) + (p < n - 1).astype(jnp.int32))

    def packet_copy(i):
        return pltpu.make_async_remote_copy(
            src_ref=packet,
            dst_ref=everyone.at[pl.ds(p * own_blocks, own_blocks)],
            send_sem=all_send,
            recv_sem=all_recv,
            device_id=place(other, peer(i)),
            device_id_type=MESH,
        )

    start(rim_copy, 0)

    @pl.loop(0, n)
    def _(i):
        packet_copy(i).start()

    own_cols[...] = own.T

    def field(targets, source_cols, count, charge, dipole):
        x, y, z = (targets[c : c + 1, :] for c in range(3))
        width = targets.shape[1]

        def step(i, sums):
            at = pl.ds(pl.multiple_of(i * 8, 8), 8)
            source = source_cols[at, :]
            rx = x - source[:, 0:1]
            ry = y - source[:, 1:2]
            rz = z - source[:, 2:3]
            w = lax.rsqrt(rx * rx + ry * ry + rz * rz + SMOOTH)
            w2 = w * w
            w3 = w2 * w
            if not dipole:
                s = charge(at, source) * w3
                return (sums[0] + rx * s, sums[1] + ry * s, sums[2] + rz * s)
            d = extra_cols[at, :]
            dx, dy, dz = d[:, 0:1], d[:, 1:2], d[:, 2:3]
            s = 3.0 * (rx * dx + ry * dy + rz * dz) * (w3 * w2)
            return (
                sums[0] + (rx * s - dx * w3),
                sums[1] + (ry * s - dy * w3),
                sums[2] + (rz * s - dz * w3),
            )

        zero = jnp.zeros((8, width), F32)
        sums = lax.fori_loop(0, count // 8, step, (zero, zero, zero), unroll=16)
        return [jnp.sum(s, axis=0, keepdims=True) for s in sums]

    def edges():
        arrive(rim_copy, 0)
        for tile in range(own_blocks):
            at = slice(tile * BLOCK, (tile + 1) * BLOCK)
            index = neighbours[:, at]
            local = index & (BLOCK - 1)
            chunk = lax.shift_right_logical(index, 7)
            picked = []
            for c in range(4):
                pieces = [
                    (b, own_rows[c : c + 1, b * BLOCK : (b + 1) * BLOCK])
                    for b in range(own_blocks)
                ] + [(own_blocks + side, rim_in[0, side, c : c + 1, :]) for side in range(2)]
                picked.append(table_gather(pieces, local, chunk))
            ox, oy, oz = (own_rows[c : c + 1, at] - picked[c] for c in range(3))
            dist_sq = ox * ox + oy * oy + oz * oz + SMOOTH
            yield at, (ox, oy, oz), dist_sq, picked[3], local, chunk

    def send_terms(charge, dipole):
        width = listed * BLOCK
        for half in range(0, width, 2 * BLOCK):
            out = field(
                near_rows[:, half : half + 2 * BLOCK], own_cols, rows, charge, dipole
            )
            for c in range(3):
                terms[c : c + 1, half : half + 2 * BLOCK] = out[c]

    centre = lax.broadcasted_iota(jnp.int32, (basis, rows), 0).astype(F32) * SPACING

    def radial_step(q, layer):
        parts = []
        for j in range(pack):
            away = jnp.broadcast_to(geometry[0, pl.ds(q * pack + j, 1), :], (basis, rows))
            away = away - centre
            parts.append(jnp.exp(-(away * away)))
        wave = jnp.concatenate(parts, axis=0).astype(BF16)
        h = lax.dot_general(
            wave, wide_in[layer], (((0,), (0,)), ((), ())), preferred_element_type=F32
        )
        h = silu(h).astype(BF16)
        for m in range(2):
            h = silu(jnp.dot(h, wide_mid[layer, m], preferred_element_type=F32)).astype(BF16)
        third[layer, q] = h

    def radial_net(layer):
        @pl.loop(0, groups, unroll=4)
        def _(q):
            radial_step(q, layer)

    def edge_net(layer):
        @pl.loop(0, pack)
        def _(j):
            weight = jnp.dot(
                third[layer].reshape(groups * rows, channels),
                wide_out[layer, j],
                preferred_element_type=F32,
            )
            edge_weight[j] = weight.reshape(groups, rows, channels)

    @pl.when(g == 0)
    def _():
        lane = lax.broadcasted_iota(jnp.int32, (rows, rows + 2 * rim), 1)
        listing = jnp.concatenate(
            [neighbours[...].astype(F32), jnp.zeros((BLOCK - slots, rows), F32)], axis=0
        ).T.astype(jnp.int32)
        for k in range(slots):
            hot[k % pack, k // pack] = jnp.where(listing[:, k : k + 1] == lane, 1.0, 0.0).astype(BF16)
        spread_r = (
            lax.broadcasted_iota(jnp.int32, (channels, radial), 0) % radial
            == lax.broadcasted_iota(jnp.int32, (channels, radial), 1)
        ).astype(F32).astype(BF16)
        spread_c = (
            lax.broadcasted_iota(jnp.int32, (radial, channels), 1) % radial
            == lax.broadcasted_iota(jnp.int32, (radial, channels), 0)
        ).astype(F32).astype(BF16)
        same_in = (
            lax.broadcasted_iota(jnp.int32, (pack * basis, channels), 0) // basis
            == lax.broadcasted_iota(jnp.int32, (pack * basis, channels), 1) // radial
        )
        same_mid = (
            lax.broadcasted_iota(jnp.int32, (channels, channels), 0) // radial
            == lax.broadcasted_iota(jnp.int32, (channels, channels), 1) // radial
        )
        for layer in range(layers):
            flat = jnp.dot(radial_in[layer], spread_c, preferred_element_type=F32)
            wide_in[layer] = jnp.where(
                same_in, jnp.concatenate([flat] * pack, axis=0), 0.0
            ).astype(BF16)
            for m in range(2):
                flat = jnp.dot(
                    jnp.dot(spread_r, radial_mid[layer, m], preferred_element_type=F32).astype(
                        BF16
                    ),
                    spread_c,
                    preferred_element_type=F32,
                )
                wide_mid[layer, m] = jnp.where(same_mid, flat, 0.0).astype(BF16)
            for j in range(pack):
                wide_out[layer, j] = jnp.zeros((channels, channels), BF16)
                wide_out[layer, j, j * radial : (j + 1) * radial, :] = radial_out[layer]
        for at, _, dist_sq, _, _, _ in edges():
            geometry[0, :, at] = jnp.sqrt(dist_sq)
        radial_net(0)

    @pl.when(g == 1)
    def _():
        for at, offset, dist_sq, source_charge, _, _ in edges():
            w = lax.rsqrt(dist_sq)
            w2 = w * w
            w3 = w2 * w
            s = source_charge * w3
            for c in range(3):
                geometry[c, :, at] = offset[c]
                extra = jnp.sum(offset[c] * s, axis=0, keepdims=True)
                pairs[c : c + 1, at] = extra
            geometry[3, :, at] = w3
            geometry[4, :, at] = 3.0 * (w3 * w2)

    pltpu.make_async_copy(everyone, everyone, all_recv).wait()
    for l in range(listed):
        tile = everyone[blocks[l]]
        near_rows[:, l * BLOCK : (l + 1) * BLOCK] = tile
        near_cols[l * BLOCK : (l + 1) * BLOCK, :] = tile.T

    out = field(own, near_cols, listed * BLOCK, lambda at, source: source[:, 3:4], False)
    for c in range(3):
        outside[c : c + 1, :] = out[c]

    @pl.when(g == 0)
    def _():
        fx, fy, fz = out
        strength = jnp.sqrt(1.0 + fx * fx + fy * fy + fz * fz)
        site_result[2:3, :] = strength
        strength_col = jnp.broadcast_to(strength, (8, rows)).T[:, 0:1]
        hidden_ref[...] = (features[...].astype(F32) + strength_col * field_gain[...]).astype(BF16)

        def lift(layer):
            lifted = jnp.dot(
                hidden_ref[...], node_in[layer], preferred_element_type=F32
            ).astype(BF16)
            site = lax.broadcasted_iota(jnp.int32, (rows, rim), 0)
            for side in range(2):
                pick = jnp.where(site == send_rows[side : side + 1, :], 1.0, 0.0).astype(BF16)
                lent[layer, side] = lax.dot_general(
                    pick, lifted, (((0,), (0,)), ((), ())), preferred_element_type=F32
                ).astype(BF16)
            start(lift_copy, layer)
            tables[layer, 0:rows] = lifted

        for layer in range(layers):
            lift(layer)
            edge_net(layer)
            if layer + 1 < layers:
                radial_net(layer + 1)
            arrive(lift_copy, layer)
            acc[...] = jnp.zeros_like(acc)

            @pl.loop(0, pack, unroll=2)
            def _(j):
                source = jnp.dot(
                    hot[j].reshape(groups * rows, rows + 2 * rim),
                    tables[layer],
                    preferred_element_type=F32,
                )
                product = edge_weight[j] * source.reshape(groups, rows, channels)
                acc[...] += jnp.sum(product, axis=0)

            message = (acc[...] * (1.0 / slots)).astype(BF16)
            update = silu(jnp.dot(message, node_out[layer], preferred_element_type=F32))
            hidden_ref[...] = (hidden_ref[...].astype(F32) + update).astype(BF16)

        across = (((1,), (1,)), ((), ()))
        extra_cols[:, 0:2] = lax.dot_general(
            hidden_ref[...], readout[...], across, preferred_element_type=F32
        )
        site_result[0:2, :] = lax.dot_general(
            readout[...], hidden_ref[...], across, preferred_element_type=F32
        )
        send_terms(lambda at, source: extra_cols[at, 0:1], False)
        for layer in range(layers):
            gone(lift_copy, layer)

    @pl.when(g == 1)
    def _():
        gain = polar[...]
        outside[...] = outside[...] + pairs[...]
        dipole = [gain * outside[c : c + 1, :] for c in range(3)]
        for sweep in range(SWEEPS):
            step = 1 + sweep
            stacked = jnp.concatenate(dipole + [jnp.zeros((5, rows), F32)], axis=0)
            fill_rims(step, stacked)
            start(rim_copy, step)
            arrive(rim_copy, step)
            fresh = [[], [], []]
            for tile in range(own_blocks):
                at = slice(tile * BLOCK, (tile + 1) * BLOCK)
                index = neighbours[:, at]
                local = index & (BLOCK - 1)
                chunk = lax.shift_right_logical(index, 7)
                d = []
                for c in range(3):
                    pieces = [
                        (b, dipole[c][:, b * BLOCK : (b + 1) * BLOCK]) for b in range(own_blocks)
                    ] + [
                        (own_blocks + side, rim_in[step, side, c : c + 1, :]) for side in range(2)
                    ]
                    d.append(table_gather(pieces, local, chunk))
                r = [geometry[c, :, at] for c in range(3)]
                w3 = geometry[3, :, at]
                s = (r[0] * d[0] + r[1] * d[1] + r[2] * d[2]) * geometry[4, :, at]
                for c in range(3):
                    total = jnp.sum(r[c] * s - d[c] * w3, axis=0, keepdims=True)
                    fresh[c].append(gain[:, at] * (outside[c : c + 1, at] + total))
            dipole = [jnp.concatenate(f, axis=1) for f in fresh]
        for c in range(3):
            site_result[c : c + 1, :] = dipole[c]
        stacked = jnp.concatenate(dipole + [jnp.zeros((5, rows), F32)], axis=0)
        extra_cols[...] = stacked.T
        send_terms(None, True)
        for sweep in range(SWEEPS):
            gone(rim_copy, 1 + sweep)

    @pl.loop(0, n)
    def _(q):
        for b in range(own_blocks):
            total = jnp.zeros((3, BLOCK), F32)
            for l in range(listed):
                total = total + jnp.where(
                    blocks[l] == q * own_blocks + b, terms[:, l * BLOCK : (l + 1) * BLOCK], 0.0
                )
            term_out[q, b * 3 : (b + 1) * 3, :] = total

    def term_copy(i):
        return pltpu.make_async_remote_copy(
            src_ref=term_out.at[peer(i)],
            dst_ref=term_in.at[p],
            send_sem=term_send,
            recv_sem=term_recv,
            device_id=place(other, peer(i)),
            device_id_type=MESH,
        )

    @pl.loop(0, n)
    def _(i):
        term_copy(i).start()

    gone(rim_copy, 0)
    pltpu.make_async_copy(everyone, everyone, all_send).wait()
    pltpu.make_async_copy(term_in, term_in, term_recv).wait()

    total = jnp.sum(term_in[...], axis=0)
    for b in range(own_blocks):
        response[:, b * BLOCK : (b + 1) * BLOCK] = total[b * 3 : (b + 1) * 3, :]
    pltpu.make_async_copy(term_in, term_in, term_send).wait()


def local(n_dom, n_sub, *args):
    (
        positions,
        charges,
        polar,
        features,
        neighbours,
        send_rows,
        blocks,
        radial_in,
        radial_mid,
        radial_out,
        node_in,
        node_out,
        field_gain,
        readout,
    ) = args
    n = n_dom * n_sub
    rows = positions.shape[1]
    own_blocks = rows // BLOCK
    slots = neighbours.shape[1]
    listed = blocks.shape[0]
    layers, basis, radial = radial_in.shape
    channels = features.shape[1]
    rim = send_rows.shape[1]
    pack = channels // radial
    vmem = pl.BlockSpec(memory_space=pltpu.VMEM)
    specs = [vmem] * 14
    specs[6] = pl.BlockSpec(memory_space=pltpu.SMEM)
    dma = pltpu.SemaphoreType.DMA
    both = pl.pallas_call(
        functools.partial(kernel, n_dom, n_sub),
        out_shape=jax.ShapeDtypeStruct((2, 3, rows), F32),
        in_specs=specs,
        out_specs=vmem,
        scratch_shapes=[
            pltpu.VMEM((own_blocks, 8, BLOCK), F32),
            pltpu.VMEM((n * own_blocks, 8, BLOCK), F32),
            pltpu.VMEM((8, listed * BLOCK), F32),
            pltpu.VMEM((listed * BLOCK, 8), F32),
            pltpu.VMEM((8, rows), F32),
            pltpu.VMEM((rows, 8), F32),
            pltpu.VMEM((rows, 8), F32),
            pltpu.VMEM((1 + SWEEPS, 2, 8, rim), F32),
            pltpu.VMEM((1 + SWEEPS, 2, 8, rim), F32),
            pltpu.VMEM((5, slots, rows), F32),
            pltpu.VMEM((pack, slots // pack, rows, rows + 2 * rim), BF16),
            pltpu.VMEM((layers, slots // pack, rows, channels), BF16),
            pltpu.VMEM((pack, slots // pack, rows, channels), F32),
            pltpu.VMEM((layers, pack * basis, channels), BF16),
            pltpu.VMEM((layers, 2, channels, channels), BF16),
            pltpu.VMEM((layers, pack, channels, channels), BF16),
            pltpu.VMEM((layers, rows + 2 * rim, channels), BF16),
            pltpu.VMEM((layers, 2, rim, channels), BF16),
            pltpu.VMEM((rows, channels), BF16),
            pltpu.VMEM((rows, channels), F32),
            pltpu.VMEM((3, rows), F32),
            pltpu.VMEM((3, rows), F32),
            pltpu.VMEM((3, listed * BLOCK), F32),
            pltpu.VMEM((n, own_blocks * 3, BLOCK), F32),
            pltpu.VMEM((n, own_blocks * 3, BLOCK), F32),
            dma(()),
            dma(()),
            dma((1 + SWEEPS, 2)),
            dma((1 + SWEEPS, 2)),
            dma((layers, 2)),
            dma((layers, 2)),
            dma(()),
            dma(()),
        ],
        compiler_params=pltpu.CompilerParams(
            collective_id=0, has_side_effects=True, vmem_limit_bytes=56 * 2**20
        ),
    )(
        positions,
        charges.reshape(1, -1),
        polar.reshape(1, -1),
        features,
        neighbours.T,
        send_rows,
        blocks,
        radial_in,
        radial_mid,
        radial_out,
        node_in,
        node_out,
        field_gain.reshape(1, -1),
        readout.T,
    )
    return both[0], both[1]


def solution(mesh):
    sites = ("grp", "dom", "sub")
    in_specs = (
        P(None, sites),
        P(sites),
        P(sites),
        P(sites, None),
        P(sites, None),
        P(None, sites),
        P(sites),
    ) + (P(),) * 7
    out_specs = (P(None, sites), P(None, sites))
    body = functools.partial(local, mesh.shape["dom"], mesh.shape["sub"])
    return jax.shard_map(body, mesh=mesh, in_specs=in_specs, out_specs=out_specs, check_vma=False)
```
